256 devices in a mesh: rad: 32 (over x, y, core), pol: 8 (over z).
Axes of the slice: x: 4, y: 4, z: 8, core: 2. Of those that a mesh axis runs over, the one named last changes fastest.
Arguments:
- dust: float32 [128, 64, 16384], P(None, 'pol', 'rad'), may hold values from 0.2 to 2
- drift_courant: float32 [128], replicated, may hold values from 0.1 to 0.6
- mixing: float32 [128], replicated, may hold values from 0.02 to 0.1
- pair_table: int32 [3, 2048], replicated, may hold values from 0 to 127
- pair_rate: float32 [2048], replicated, may hold values from 0.002 to 0.02
- absorption: float32 [128, 128], replicated, may hold values from 0.05 to 5
- stellar_flux: float32 [128], replicated, may hold values from 0.01 to 0.1
- band_channel: int32 [128], replicated, may hold values from 0 to 3
Outputs:
- new_dust: float32 [128, 64, 16384], P(None, 'pol', 'rad')
- heating: float32 [4, 64, 16384], P(None, 'pol', 'rad')
The draws below stay inside these ranges and needn't reach their ends.
Inputs may be any that keep to these rules, and one draw needn't show every extreme that they name: `pair_table`: sizes of dust.
All inputs are finite; a program needn't handle non-finite values.
Results may differ from the reference program's by a relative error of at most 0.00005.
Values sent between devices are 32-bit elements; how exact they have to be, the bound alone decides.
A program may use at most 192 MiB of HBM per device.

```python
import math
from functools import partial
import jax
import jax.numpy as jnp
from jax import lax

S = 128
B = 128
PAIRS = 2048
CH = 4
CR = 512
NR = 16384
NT = 64
N_RAD = 32


def touch_ends(entries, key, least, largest):
    index_at = [jax.random.randint(jax.random.fold_in(key, axis), (), 0, length) for axis, length in enumerate(entries.shape)]
    main_axis = entries.shape.index(max(entries.shape))
    neighbour = index_at[:main_axis] + [(index_at[main_axis] + 1) % entries.shape[main_axis]] + index_at[main_axis + 1:]
    return entries.at[tuple(index_at)].set(least).at[tuple(neighbour)].set(largest)


def block_levels(key, dims, pieces, least, top_value):
    def one(position, shards_of):
        steps = jax.random.uniform(jax.random.fold_in(jax.random.fold_in(key, 6), position), (shards_of,), jnp.float32, least / len(pieces), top_value / len(pieces))
        return jnp.repeat(jnp.exp(steps), dims[position] // shards_of).reshape((-1,) + (1,) * (len(dims) - position - 1))

    factor_of = one(*pieces[0])
    for cut in pieces[1:]:
        factor_of = factor_of * one(*cut)
    return factor_of


def setup_inputs(seed: int = 0) -> dict:
    splits = jax.random.split(jax.random.key(seed), 9)
    dust = jnp.clip(jnp.exp(math.log(2.0) - 2.3025851 * jax.random.uniform(splits[0], (S, NT, NR), jnp.float32) ** block_levels(splits[0], (S, NT, NR), ((1, 8), (2, 32)), -0.2, 0.2)), 0.2, 2.0)
    drift_courant = jnp.clip(jnp.exp(jax.random.uniform(splits[1], (S,), jnp.float32, math.log(0.1), math.log(0.6))), 0.1, 0.6)
    mixing = jnp.clip(jnp.exp(jax.random.uniform(splits[2], (S,), jnp.float32, math.log(0.02), math.log(0.1))), 0.02, 0.1)
    pair_table = touch_ends(jax.random.randint(splits[3], (3, PAIRS), 0, S), jax.random.fold_in(splits[3], 1), 0, S - 1).astype(jnp.int32)
    pair_rate = jnp.clip(jnp.exp(jax.random.uniform(splits[4], (PAIRS,), jnp.float32, math.log(0.002), math.log(0.02))), 0.002, 0.02)
    absorption = jnp.clip(jnp.exp(jax.random.uniform(splits[5], (B, S), jnp.float32, math.log(0.05), math.log(5.0))), 0.05, 5.0)
    stellar_flux = jnp.clip(jnp.exp(jax.random.uniform(splits[6], (B,), jnp.float32, math.log(0.01), math.log(0.1))), 0.01, 0.1)
    band_channel = touch_ends(jax.random.randint(splits[7], (B,), 0, CH), jax.random.fold_in(splits[7], 1), 0, CH - 1).astype(jnp.int32)
    return {"dust": dust, "drift_courant": drift_courant, "mixing": mixing, "pair_table": pair_table, "pair_rate": pair_rate, "absorption": absorption, "stellar_flux": stellar_flux, "band_channel": band_channel}


depth_scale = 4.0


def collide_block(pair_table, pair_rate, block):
    first = pair_table[0]
    second = pair_table[1]
    target = pair_table[2]
    product = pair_rate[:, None, None] * block[first] * block[second]
    change = jax.ops.segment_sum(product, target, num_segments=S)
    change = change - jax.ops.segment_sum(product, first, num_segments=S)
    change = change - jax.ops.segment_sum(product, second, num_segments=S)
    return block + change


def reference(dust, drift_courant, mixing, pair_table, pair_rate, absorption, stellar_flux, band_channel):
    padded = jnp.pad(dust, ((0, 0), (1, 1), (1, 1)))
    center = padded[:, 1:-1, 1:-1]
    outer = padded[:, 1:-1, 2:]
    inner = padded[:, 1:-1, :-2]
    upper = padded[:, 2:, 1:-1]
    lower = padded[:, :-2, 1:-1]
    drift = drift_courant[:, None, None]
    spread = mixing[:, None, None]
    advected = center + drift * (outer - center) + spread * (outer + inner + upper + lower - 4.0 * center)
    blocks = jnp.moveaxis(advected.reshape(S, NT, N_RAD, CR), 2, 0)
    collided = lax.map(partial(collide_block, pair_table, pair_rate), blocks)
    new_dust = jnp.moveaxis(collided, 0, 2).reshape(S, NT, NR)
    opacity = jnp.einsum('bs,str->btr', absorption, new_dust, precision=lax.Precision.HIGHEST) / S
    step_depth = opacity * (depth_scale / NR)
    depth = jnp.cumsum(step_depth, axis=2) - step_depth
    absorbed = stellar_flux[:, None, None] * jnp.exp(-depth) * (-jnp.expm1(-step_depth)) * NR
    picker = (jnp.arange(CH, dtype=jnp.int32)[:, None] == band_channel[None, :]).astype(jnp.float32)
    heating = jnp.einsum('cb,btr->ctr', picker, absorbed, precision=lax.Precision.HIGHEST)
    return new_dust, heating
```

```python
import functools

import jax
import jax.numpy as jnp
from jax import lax
from jax.experimental import pallas as pl
from jax.experimental.pallas import tpu as pltpu
from jax.sharding import PartitionSpec as P

CH = 4
LANES = 128
SUB = 8
depth_scale = 4.0
SHIFT = 10.0
UNROLL = 16
f32 = jnp.float32
bf16 = jnp.bfloat16


def halves(x):
    hi = x.astype(bf16)
    return hi, (x - hi.astype(f32)).astype(bf16)


def dot_nt(a, b):
    return lax.dot_general(a, b, (((1,), (1,)), ((), ())), preferred_element_type=f32)


def stacked(matrix):
    hi, lo = halves(matrix)
    return jnp.concatenate(
        [jnp.concatenate([hi, hi], axis=1), jnp.concatenate([lo, lo], axis=1)], axis=0
    )


def product(left, right):
    rows = left.shape[0] // 2
    both = jnp.dot(
        left, jnp.concatenate(halves(right), axis=0), preferred_element_type=f32
    )
    return both[:rows] + both[rows:]


def halo_kernel(
    n_rad, n_pol, dust, table, rate, below, above, left, right, rows_at, loss,
    ends, sent, load_sem, send_sem, recv_sem,
):
    sizes = dust.shape[0]
    tile = dust.shape[2]
    rad = lax.axis_index("rad")
    pol = lax.axis_index("pol")
    rad_up, rad_down = lax.rem(rad + 1, n_rad), lax.rem(rad + n_rad - 1, n_rad)
    pol_up, pol_down = lax.rem(pol + 1, n_pol), lax.rem(pol + n_pol - 1, n_pol)
    barrier = pltpu.get_barrier_semaphore()
    pl.semaphore_signal(barrier, inc=1, device_id={"rad": rad_up})
    pl.semaphore_signal(barrier, inc=1, device_id={"rad": rad_down})
    pl.semaphore_signal(barrier, inc=1, device_id={"pol": pol_up})
    pl.semaphore_signal(barrier, inc=1, device_id={"pol": pol_down})
    loads = [
        pltpu.make_async_copy(dust.at[:, :, pl.ds(0, LANES)], ends.at[0], load_sem.at[0]),
        pltpu.make_async_copy(
            dust.at[:, :, pl.ds(tile - LANES, LANES)], ends.at[1], load_sem.at[1]
        ),
    ]
    for load in loads:
        load.start()
    pl.semaphore_wait(barrier, 4)
    copies = [
        pltpu.make_async_remote_copy(
            dust.at[:, SUB - 1, :], below, send_sem.at[0], recv_sem.at[0],
            device_id={"pol": pol_up},
        ),
        pltpu.make_async_remote_copy(
            dust.at[:, 0, :], above, send_sem.at[1], recv_sem.at[1],
            device_id={"pol": pol_down},
        ),
    ]
    for copy in copies:
        copy.start()
    for load in loads:
        load.wait()
    lane = lax.broadcasted_iota(jnp.int32, (SUB, LANES), 1)

    def gather(group, carry):
        first, last = carry
        for step in range(8):
            size = group * 8 + step
            here = lane == size
            first = jnp.where(here, ends[0, size][:, 0:1], first)
            last = jnp.where(here, ends[1, size][:, LANES - 1 :], last)
        return first, last

    zero = jnp.zeros((SUB, LANES), f32)
    first, last = lax.fori_loop(0, sizes // 8, gather, (zero, zero))
    sent[0] = first
    sent[1] = last
    for piece in range(table.shape[1] // LANES):
        for row in range(3):
            rows_at[pl.ds(row * (table.shape[1] // LANES) + piece, 1), :] = (
                table[row : row + 1, LANES * piece : LANES * piece + LANES] * (4 * SUB)
            )
    edges = [
        pltpu.make_async_remote_copy(
            sent.at[1], left, send_sem.at[2], recv_sem.at[2], device_id={"rad": rad_up}
        ),
        pltpu.make_async_remote_copy(
            sent.at[0], right, send_sem.at[3], recv_sem.at[3], device_id={"rad": rad_down}
        ),
    ]
    for copy in edges:
        copy.start()

    grid = lax.broadcasted_iota(jnp.int32, (sizes, LANES), 0)
    total = jnp.zeros((sizes, sizes), f32)
    for piece in range(table.shape[1] // LANES):
        cut = slice(LANES * piece, LANES * piece + LANES)
        is_first = grid == table[0:1, cut]
        is_second = grid == table[1:2, cut]
        rates = rate[piece : piece + 1, :]
        ones = jnp.concatenate([is_second, is_first], axis=1).astype(f32).astype(bf16)
        weights = jnp.concatenate(
            [jnp.where(is_first, rates, 0.0), jnp.where(is_second, rates, 0.0)], axis=1
        )
        high, rest = halves(weights)
        total = total + dot_nt(high, ones) + dot_nt(rest, ones)
    loss[...] = total
    for copy in copies + edges:
        copy.wait()


def collide_kernel(
    n_rad, n_pol, dust, below, above, left, right, drift, mixing, rows_at, rate, loss,
    out, adv, gain_a, gain_b,
):
    sizes = dust.shape[0]
    pairs = rate.shape[0]
    pieces = dust.shape[2] // LANES
    span = pieces * SUB
    rad = lax.axis_index("rad")
    pol = lax.axis_index("pol")
    lane = lax.broadcasted_iota(jnp.int32, (SUB, LANES), 1)
    sub = lax.broadcasted_iota(jnp.int32, (SUB, LANES), 0)
    has_left = jnp.where(rad > 0, 1.0, 0.0)
    has_right = jnp.where(rad < n_rad - 1, 1.0, 0.0)
    has_below = jnp.where(pol > 0, 1.0, 0.0)
    has_above = jnp.where(pol < n_pol - 1, 1.0, 0.0)
    zero = jnp.zeros((SUB, LANES), f32)

    def advect(group, carry):
        at_left, at_right = carry
        for step in range(4):
            size = group * 4 + step
            c = drift[size]
            m = mixing[size]
            center = dust[size]
            cells = [center[:, LANES * k : LANES * k + LANES] for k in range(pieces)]
            back = [pltpu.roll(x, LANES - 1, 1) for x in cells] + [at_right]
            forth = [at_left] + [pltpu.roll(x, 1, 1) for x in cells]
            low_row = below[pl.ds(size, 1), :] * has_below
            high_row = above[pl.ds(size, 1), :] * has_above
            for k in range(pieces):
                cut = slice(LANES * k, LANES * k + LANES)
                here = cells[k]
                outer = jnp.where(lane == LANES - 1, back[k + 1], back[k])
                inner = jnp.where(lane == 0, forth[k], forth[k + 1])
                upper = jnp.where(sub == SUB - 1, high_row[:, cut], pltpu.roll(here, SUB - 1, 0))
                lower = jnp.where(sub == 0, low_row[:, cut], pltpu.roll(here, 1, 0))
                value = (
                    here
                    + c * (outer - here)
                    + m * (outer + inner + upper + lower - 4.0 * here)
                )
                rows = pl.ds(pl.multiple_of(size * span + k * SUB, SUB), SUB)
                adv[rows, :] = value
                gain_a[rows, :] = value
                gain_b[rows, :] = zero
            at_left = pltpu.roll(at_left, LANES - 1, 1)
            at_right = pltpu.roll(at_right, LANES - 1, 1)
        return at_left, at_right

    lax.fori_loop(
        0,
        sizes // 4,
        advect,
        (left[...] * has_left, pltpu.roll(right[...] * has_right, LANES - 1, 1)),
    )

    def rows(start):
        return pl.ds(pl.multiple_of(start, span), span)

    def collide(group, _):
        base = group * UNROLL
        for step in range(UNROLL):
            first = rows_at[base + step]
            second = rows_at[base + (pairs + step)]
            target = rows_at[base + (2 * pairs + step)]
            value = (rate[base + step] * adv[rows(first), :]) * adv[rows(second), :]
            gain = gain_a if step % 2 == 0 else gain_b
            gain[rows(target), :] = gain[rows(target), :] + value
        return 0

    lax.fori_loop(0, pairs // UNROLL, collide, 0)

    matrix = stacked(loss[...])
    for t in range(SUB):
        parts = [pl.ds(k * SUB + t, sizes, stride=span) for k in range(pieces)]
        here = jnp.concatenate([adv[part, :] for part in parts], axis=1)
        lost = here * product(matrix, here)
        for k in range(pieces):
            cut = slice(LANES * k, LANES * k + LANES)
            out[:, t, cut] = gain_a[parts[k], :] + gain_b[parts[k], :] - lost[:, cut]


def heat_kernel(
    n_rad, dust, absorption, flux, channel, heating,
    steps, factor, tile_total, arrived, send_sem, recv_sem,
):
    sizes = dust.shape[0]
    tile = dust.shape[2]
    bands = absorption.shape[0]
    pieces = tile // LANES
    ray_length = tile * n_rad
    rad = lax.axis_index("rad")
    barrier = pltpu.get_barrier_semaphore()

    def greet(away, _):
        pl.semaphore_signal(barrier, inc=1, device_id={"rad": lax.rem(rad + away, n_rad)})
        return 0

    lax.fori_loop(1, n_rad, greet, 0)

    matrix = stacked(absorption[...] * (depth_scale / (ray_length * sizes)))
    lane = lax.broadcasted_iota(jnp.int32, (bands, LANES), 1)
    column = jnp.zeros((bands, LANES), f32)
    for t in range(SUB):
        step = product(matrix, dust[:, t, :])
        steps[t] = step
        over = step[:, :LANES]
        for k in range(1, pieces):
            over = over + step[:, LANES * k : LANES * k + LANES]
        column = jnp.where(lane == t, jnp.sum(over, axis=1, keepdims=True), column)
    tile_total[...] = jnp.transpose(column)[:SUB]
    pl.semaphore_wait(barrier, n_rad - 1)

    def send(away, _):
        pltpu.make_async_remote_copy(
            tile_total, arrived.at[away - 1], send_sem, recv_sem,
            device_id={"rad": lax.rem(rad + away, n_rad)},
        ).start()
        return 0

    lax.fori_loop(1, n_rad, send, 0)

    row = lax.broadcasted_iota(jnp.int32, (LANES, LANES), 0)
    col = lax.broadcasted_iota(jnp.int32, (LANES, LANES), 1)
    ahead = jnp.concatenate(
        [jnp.where(row < col, 1.0, 0.0), jnp.ones((LANES, LANES), f32)], axis=1
    ).astype(bf16)
    ahead = jnp.concatenate([ahead, ahead], axis=0)
    for t in range(SUB):
        so_far = jnp.zeros((bands, LANES), f32)
        for k in range(pieces):
            cut = slice(LANES * k, LANES * k + LANES)
            x = steps[t, :, cut]
            sums = jnp.dot(
                jnp.concatenate(halves(x), axis=1), ahead, preferred_element_type=f32
            )
            within = so_far + sums[:, :LANES]
            so_far = so_far + sums[:, LANES:]
            series = x * (
                1.0 - x * (0.5 - x * (1.0 / 6 - x * (1.0 / 24 - x * (1.0 / 120 - x * (1.0 / 720)))))
            )
            taken = jnp.where(jnp.abs(x) < 0.1, series, 1.0 - jnp.exp(-x))
            high, low = halves(jnp.exp(SHIFT - within) * taken * ray_length)
            factor[t, 0:bands, cut] = high
            factor[t, bands : 2 * bands, cut] = low

    pltpu.make_async_copy(arrived, arrived, recv_sem).wait()
    offset = jnp.zeros((SUB, bands), f32)
    for away in range(1, n_rad):
        offset = offset + jnp.where(rad >= away, arrived[away - 1], 0.0)
    weight = flux[...] * jnp.exp(-offset - SHIFT)
    which = lax.broadcasted_iota(jnp.int32, (SUB, bands), 0) == channel[...]
    for t in range(SUB):
        high, low = halves(jnp.where(which, weight[t : t + 1, :], 0.0))
        left = jnp.concatenate(
            [jnp.concatenate([high, high], axis=1), jnp.concatenate([low, low], axis=1)], axis=0
        )
        both = jnp.dot(left, factor[t], preferred_element_type=f32)
        heating[:, t, :] = (both[:SUB] + both[SUB:])[:CH]
    pltpu.make_async_copy(arrived, arrived, send_sem).wait()


VMEM = pl.BlockSpec(memory_space=pltpu.VMEM)
SMEM = pl.BlockSpec(memory_space=pltpu.SMEM)
ANY = pl.BlockSpec(memory_space=pl.ANY)


def shards(
    dust, drift_courant, mixing, pair_table, pair_rate, absorption, stellar_flux, band_channel
):
    n_rad = lax.axis_size("rad")
    n_pol = lax.axis_size("pol")
    sizes, rows, tile = dust.shape
    pairs = pair_rate.shape[0]
    bands = absorption.shape[0]
    pieces = tile // LANES

    def like(*shape, dtype=f32):
        return jax.ShapeDtypeStruct(shape, dtype)

    below, above, left, right, rows_at, loss = pl.pallas_call(
        functools.partial(halo_kernel, n_rad, n_pol),
        out_shape=(
            like(sizes, tile),
            like(sizes, tile),
            like(rows, sizes),
            like(rows, sizes),
            like(3 * pairs // LANES, LANES, dtype=jnp.int32),
            like(sizes, sizes),
        ),
        in_specs=[ANY, VMEM, VMEM],
        out_specs=(VMEM,) * 6,
        scratch_shapes=[
            pltpu.VMEM((2, sizes, rows, LANES), f32),
            pltpu.VMEM((2, rows, sizes), f32),
            pltpu.SemaphoreType.DMA((2,)),
            pltpu.SemaphoreType.DMA((4,)),
            pltpu.SemaphoreType.DMA((4,)),
        ],
        compiler_params=pltpu.CompilerParams(collective_id=0, has_side_effects=True),
        name="halo",
    )(dust, pair_table, pair_rate.reshape(pairs // LANES, LANES))
    new_dust = pl.pallas_call(
        functools.partial(collide_kernel, n_rad, n_pol),
        out_shape=like(sizes, rows, tile),
        in_specs=[VMEM] * 5 + [SMEM] * 4 + [VMEM],
        out_specs=VMEM,
        scratch_shapes=[pltpu.VMEM((sizes * pieces * SUB, LANES), f32)] * 3,
        name="collide",
    )(
        dust, below, above, left, right, drift_courant, mixing,
        rows_at.reshape(3 * pairs), pair_rate, loss,
    )
    heating = pl.pallas_call(
        functools.partial(heat_kernel, n_rad),
        out_shape=like(CH, rows, tile),
        in_specs=[VMEM] * 4,
        out_specs=VMEM,
        scratch_shapes=[
            pltpu.VMEM((rows, bands, tile), f32),
            pltpu.VMEM((rows, 2 * bands, tile), bf16),
            pltpu.VMEM((rows, bands), f32),
            pltpu.VMEM((n_rad - 1, rows, bands), f32),
            pltpu.SemaphoreType.DMA,
            pltpu.SemaphoreType.DMA,
        ],
        compiler_params=pltpu.CompilerParams(collective_id=1, has_side_effects=True),
        name="heat",
    )(new_dust, absorption, stellar_flux.reshape(1, bands), band_channel.reshape(1, bands))
    return new_dust, heating


def solution(mesh):
    placed = (P(None, "pol", "rad"), P(), P(), P(), P(), P(), P(), P())
    return jax.shard_map(
        shards,
        mesh=mesh,
        in_specs=placed,
        out_specs=(P(None, "pol", "rad"), P(None, "pol", "rad")),
        check_vma=False,
    )
```

```python
import functools

import jax
import jax.numpy as jnp
from jax import lax
from jax.experimental import pallas as pl
from jax.experimental.pallas import tpu as pltpu
from jax.sharding import PartitionSpec as P

CH = 4
LANES = 128
SUB = 8
depth_scale = 4.0
SHIFT = 10.0
UNROLL = 32
GROUP = 4
f32 = jnp.float32
bf16 = jnp.bfloat16


def halves(x):
    hi = x.astype(bf16)
    return hi, (x - hi.astype(f32)).astype(bf16)


def dot_nt(a, b):
    return lax.dot_general(a, b, (((1,), (1,)), ((), ())), preferred_element_type=f32)


def stacked(matrix):
    hi, lo = halves(matrix)
    return jnp.concatenate(
        [jnp.concatenate([hi, hi], axis=1), jnp.concatenate([lo, lo], axis=1)], axis=0
    )


def product(left, right):
    rows = left.shape[0] // 2
    both = jnp.dot(
        left, jnp.concatenate(halves(right), axis=0), preferred_element_type=f32
    )
    return both[:rows] + both[rows:]


def halo_kernel(
    n_rad, n_pol, dust, table, rate, below, above, left, right, sources, targets, loss,
    ends, sent, load_sem, send_sem, recv_sem,
):
    sizes = dust.shape[0]
    tile = dust.shape[2]
    rad = lax.axis_index("rad")
    pol = lax.axis_index("pol")
    rad_up, rad_down = lax.rem(rad + 1, n_rad), lax.rem(rad + n_rad - 1, n_rad)
    pol_up, pol_down = lax.rem(pol + 1, n_pol), lax.rem(pol + n_pol - 1, n_pol)
    barrier = pltpu.get_barrier_semaphore()
    pl.semaphore_signal(barrier, inc=1, device_id={"rad": rad_up})
    pl.semaphore_signal(barrier, inc=1, device_id={"rad": rad_down})
    pl.semaphore_signal(barrier, inc=1, device_id={"pol": pol_up})
    pl.semaphore_signal(barrier, inc=1, device_id={"pol": pol_down})
    loads = [
        pltpu.make_async_copy(dust.at[:, :, pl.ds(0, LANES)], ends.at[0], load_sem.at[0]),
        pltpu.make_async_copy(
            dust.at[:, :, pl.ds(tile - LANES, LANES)], ends.at[1], load_sem.at[1]
        ),
    ]
    for load in loads:
        load.start()
    pl.semaphore_wait(barrier, 4)
    copies = [
        pltpu.make_async_remote_copy(
            dust.at[:, SUB - 1, :], below, send_sem.at[0], recv_sem.at[0],
            device_id={"pol": pol_up},
        ),
        pltpu.make_async_remote_copy(
            dust.at[:, 0, :], above, send_sem.at[1], recv_sem.at[1],
            device_id={"pol": pol_down},
        ),
    ]
    for copy in copies:
        copy.start()
    for load in loads:
        load.wait()
    lane = lax.broadcasted_iota(jnp.int32, (SUB, LANES), 1)

    def gather(group, carry):
        first, last = carry
        for step in range(8):
            size = group * 8 + step
            here = lane == size
            first = jnp.where(here, ends[0, size][:, 0:1], first)
            last = jnp.where(here, ends[1, size][:, LANES - 1 :], last)
        return first, last

    zero = jnp.zeros((SUB, LANES), f32)
    first, last = lax.fori_loop(0, sizes // 8, gather, (zero, zero))
    sent[0] = first
    sent[1] = last
    for piece in range(table.shape[1] // LANES):
        cut = slice(LANES * piece, LANES * piece + LANES)
        at = pl.ds(piece, 1)
        span = tile // LANES * SUB
        sources[at, :] = table[0:1, cut] * (span << 16) + table[1:2, cut] * span
        targets[at, :] = table[2:3, cut] * span
    edges = [
        pltpu.make_async_remote_copy(
            sent.at[1], left, send_sem.at[2], recv_sem.at[2], device_id={"rad": rad_up}
        ),
        pltpu.make_async_remote_copy(
            sent.at[0], right, send_sem.at[3], recv_sem.at[3], device_id={"rad": rad_down}
        ),
    ]
    for copy in edges:
        copy.start()

    grid = lax.broadcasted_iota(jnp.int32, (sizes, LANES), 0)
    total = jnp.zeros((sizes, sizes), f32)
    for piece in range(table.shape[1] // LANES):
        cut = slice(LANES * piece, LANES * piece + LANES)
        is_first = grid == table[0:1, cut]
        is_second = grid == table[1:2, cut]
        rates = rate[piece : piece + 1, :]
        ones = jnp.concatenate([is_second, is_first], axis=1).astype(f32).astype(bf16)
        weights = jnp.concatenate(
            [jnp.where(is_first, rates, 0.0), jnp.where(is_second, rates, 0.0)], axis=1
        )
        high, rest = halves(weights)
        total = total + dot_nt(high, ones) + dot_nt(rest, ones)
    loss[...] = total
    for copy in copies + edges:
        copy.wait()


def collide_kernel(
    n_rad, n_pol, dust, below, above, left, right, drift, mixing, sources, targets, rate, loss,
    out, turned, padded, adv, gain_a, gain_b, gain_c, gain_d, matrices, lost,
    load_sem, turn_sem, out_sem,
):
    sizes, _, tile = dust.shape
    pairs = rate.shape[0]
    pieces = tile // LANES
    span = pieces * SUB
    rad = lax.axis_index("rad")
    pol = lax.axis_index("pol")
    loads = []
    for k in range(pieces):
        cut = pl.ds(LANES * k, LANES)
        for n, (source, place) in enumerate(
            (
                (dust.at[:, :, cut], padded.at[k, :, pl.ds(1, SUB), :]),
                (below.at[:, cut], padded.at[k, :, 0, :]),
                (above.at[:, cut], padded.at[k, :, SUB + 1, :]),
            )
        ):
            load = pltpu.make_async_copy(source, place, load_sem.at[3 * k + n])
            load.start()
            loads.append(load)
    lane = lax.broadcasted_iota(jnp.int32, (SUB, LANES), 1)
    sub = lax.broadcasted_iota(jnp.int32, (SUB, LANES), 0)
    no_lower = jnp.logical_and(sub == 0, pol == 0)
    no_upper = jnp.logical_and(sub == SUB - 1, pol == n_pol - 1)
    has_left = jnp.where(rad > 0, 1.0, 0.0)
    has_right = jnp.where(rad < n_rad - 1, 1.0, 0.0)
    matrix = stacked(loss[...])

    def rows(start):
        return pl.ds(pl.multiple_of(start, span), span)

    def clear(size, _):
        for gain in (gain_b, gain_c, gain_d):
            gain[rows(size * span), :] = jnp.zeros((span, LANES), f32)
        return 0

    lax.fori_loop(0, sizes, clear, 0, unroll=4)
    for load in loads:
        load.wait()

    def advect(group, carry):
        for step in range(GROUP):
            size = group * GROUP + step
            at_left, at_right = (
                carry if step == 0 else [pltpu.roll(x, LANES - step, 1) for x in carry]
            )
            c = drift[size]
            m = mixing[size]
            cells = [padded[k, size, 1 : SUB + 1, :] for k in range(pieces)]
            back = [pltpu.roll(x, LANES - 1, 1) for x in cells] + [at_right]
            forth = [at_left] + [pltpu.roll(x, 1, 1) for x in cells]
            for k in range(pieces):
                here = cells[k]
                outer = jnp.where(lane == LANES - 1, back[k + 1], back[k])
                inner = jnp.where(lane == 0, forth[k], forth[k + 1])
                upper = jnp.where(no_upper, 0.0, padded[k, size, 2 : SUB + 2, :])
                lower = jnp.where(no_lower, 0.0, padded[k, size, 0:SUB, :])
                value = (
                    here
                    + c * (outer - here)
                    + m * (outer + inner + upper + lower - 4.0 * here)
                )
                rows = pl.ds(pl.multiple_of(size * span + k * SUB, SUB), SUB)
                adv[rows, :] = value
                gain_a[rows, :] = value
        return tuple(pltpu.roll(x, LANES - GROUP, 1) for x in carry)

    lax.fori_loop(
        0,
        sizes // GROUP,
        advect,
        (left[...] * has_left, pltpu.roll(right[...] * has_right, LANES - 1, 1)),
    )
    by_size = adv.reshape(sizes, span, LANES)
    lost_by_size = lost.reshape(sizes, span, LANES)
    gains = (gain_a, gain_b, gain_c, gain_d)
    leave = pltpu.make_async_copy(by_size, turned, turn_sem.at[0])
    leave.start()

    def collide(group, _):
        base = group * UNROLL
        for step in range(UNROLL):
            both = sources[base + step]
            first = lax.shift_right_logical(both, 16)
            second = lax.bitwise_and(both, 0xFFFF)
            target = targets[base + step]
            value = (rate[base + step] * adv[rows(first), :]) * adv[rows(second), :]
            gain = gains[step % 4]
            gain[rows(target), :] = gain[rows(target), :] + value
        return 0

    quarter = pairs // UNROLL // 4

    def collide_quarter(n):
        lax.fori_loop(n * quarter, (n + 1) * quarter, collide, 0)

    collide_quarter(0)
    leave.wait()

    def turn(row, _):
        pltpu.make_async_copy(turned.at[:, row, :], matrices.at[row], turn_sem.at[1]).start()
        return 0

    lax.fori_loop(0, span, turn, 0)
    collide_quarter(1)
    pltpu.make_async_copy(matrices, matrices, turn_sem.at[1]).wait()
    for row in range(0, span, 2):
        here = jnp.concatenate([matrices[row], matrices[row + 1]], axis=1)
        rate_lost = product(matrix, here)
        matrices[row] = rate_lost[:, :LANES]
        matrices[row + 1] = rate_lost[:, LANES:]

    def turn_back(row, _):
        pltpu.make_async_copy(matrices.at[row], turned.at[:, row, :], turn_sem.at[2]).start()
        return 0

    lax.fori_loop(0, span, turn_back, 0)
    collide_quarter(2)
    pltpu.make_async_copy(matrices, matrices, turn_sem.at[2]).wait()
    back = pltpu.make_async_copy(turned, lost_by_size, turn_sem.at[3])
    back.start()
    collide_quarter(3)
    back.wait()
    chunk = sizes // 4
    stores = []
    for part in range(4):

        def combine(size, _):
            for k in range(pieces):
                at = pl.ds(pl.multiple_of(size * span + k * SUB, SUB), SUB)
                padded[k, size, 0:SUB, :] = (
                    (gain_a[at, :] + gain_b[at, :])
                    + (gain_c[at, :] + gain_d[at, :])
                    - adv[at, :] * lost[at, :]
                )
            return 0

        lax.fori_loop(part * chunk, part * chunk + chunk, combine, 0, unroll=4)
        for k in range(pieces):
            some = pl.ds(part * chunk, chunk)
            store = pltpu.make_async_copy(
                padded.at[k, some, pl.ds(0, SUB), :],
                out.at[some, :, pl.ds(LANES * k, LANES)],
                out_sem.at[part * pieces + k],
            )
            store.start()
            stores.append(store)
    for store in stores:
        store.wait()


def heat_kernel(
    n_rad, dust, absorption, flux, channel, heating,
    natural, steps, factor, tile_total, arrived, load_sem, send_sem, recv_sem,
):
    sizes = dust.shape[0]
    tile = dust.shape[2]
    bands = absorption.shape[0]
    pieces = tile // LANES
    ray_length = tile * n_rad
    rad = lax.axis_index("rad")
    loads = []
    for t in range(SUB):
        load = pltpu.make_async_copy(dust.at[:, t, :], natural.at[t], load_sem.at[t])
        load.start()
        loads.append(load)
    barrier = pltpu.get_barrier_semaphore()

    def greet(away, _):
        pl.semaphore_signal(barrier, inc=1, device_id={"rad": lax.rem(rad + away, n_rad)})
        return 0

    lax.fori_loop(1, n_rad, greet, 0)

    matrix = stacked(absorption[...] * (depth_scale / (ray_length * sizes)))
    lane = lax.broadcasted_iota(jnp.int32, (bands, LANES), 1)
    column = jnp.zeros((bands, LANES), f32)
    for t in range(SUB):
        loads[t].wait()
        step = product(matrix, natural[t])
        steps[t] = step
        over = step[:, :LANES]
        for k in range(1, pieces):
            over = over + step[:, LANES * k : LANES * k + LANES]
        column = jnp.where(lane == t, jnp.sum(over, axis=1, keepdims=True), column)
    tile_total[...] = jnp.transpose(column)[:SUB]
    pl.semaphore_wait(barrier, n_rad - 1)

    def send(away, _):
        pltpu.make_async_remote_copy(
            tile_total, arrived.at[away - 1], send_sem, recv_sem,
            device_id={"rad": lax.rem(rad + away, n_rad)},
        ).start()
        return 0

    lax.fori_loop(1, n_rad, send, 0)

    row = lax.broadcasted_iota(jnp.int32, (LANES, LANES), 0)
    col = lax.broadcasted_iota(jnp.int32, (LANES, LANES), 1)
    ahead = jnp.concatenate(
        [jnp.where(row < col, 1.0, 0.0), jnp.ones((LANES, LANES), f32)], axis=1
    ).astype(bf16)
    ahead = jnp.concatenate([ahead, ahead], axis=0)
    for t in range(SUB):
        so_far = jnp.zeros((bands, LANES), f32)
        for k in range(pieces):
            cut = slice(LANES * k, LANES * k + LANES)
            x = steps[t, :, cut]
            sums = jnp.dot(
                jnp.concatenate(halves(x), axis=1), ahead, preferred_element_type=f32
            )
            within = so_far + sums[:, :LANES]
            so_far = so_far + sums[:, LANES:]
            taken = x * (1.0 - x * (0.5 - x * (1.0 / 6 - x * (1.0 / 24 - x * (1.0 / 120)))))
            high, low = halves(jnp.exp(SHIFT - within) * (taken * ray_length))
            factor[t, 0:bands, cut] = high
            factor[t, bands : 2 * bands, cut] = low

    pltpu.make_async_copy(arrived, arrived, recv_sem).wait()
    offset = jnp.zeros((SUB, bands), f32)
    for away in range(1, n_rad):
        offset = offset + jnp.where(rad >= away, arrived[away - 1], 0.0)
    weight = flux[...] * jnp.exp(-offset - SHIFT)
    which = lax.broadcasted_iota(jnp.int32, (SUB, bands), 0) == channel[...]
    for t in range(SUB):
        high, low = halves(jnp.where(which, weight[t : t + 1, :], 0.0))
        left = jnp.concatenate(
            [jnp.concatenate([high, high], axis=1), jnp.concatenate([low, low], axis=1)], axis=0
        )
        both = jnp.dot(left, factor[t], preferred_element_type=f32)
        heating[:, t, :] = (both[:SUB] + both[SUB:])[:CH]
    pltpu.make_async_copy(arrived, arrived, send_sem).wait()


VMEM = pl.BlockSpec(memory_space=pltpu.VMEM)
SMEM = pl.BlockSpec(memory_space=pltpu.SMEM)
ANY = pl.BlockSpec(memory_space=pl.ANY)


def shards(
    dust, drift_courant, mixing, pair_table, pair_rate, absorption, stellar_flux, band_channel
):
    n_rad = lax.axis_size("rad")
    n_pol = lax.axis_size("pol")
    sizes, rows, tile = dust.shape
    pairs = pair_rate.shape[0]
    bands = absorption.shape[0]
    pieces = tile // LANES
    span = pieces * SUB

    def like(*shape, dtype=f32):
        return jax.ShapeDtypeStruct(shape, dtype)

    below, above, left, right, sources, targets, loss = pl.pallas_call(
        functools.partial(halo_kernel, n_rad, n_pol),
        out_shape=(
            like(sizes, tile),
            like(sizes, tile),
            like(rows, sizes),
            like(rows, sizes),
            like(pairs // LANES, LANES, dtype=jnp.int32),
            like(pairs // LANES, LANES, dtype=jnp.int32),
            like(sizes, sizes),
        ),
        in_specs=[ANY, VMEM, VMEM],
        out_specs=(VMEM,) * 7,
        scratch_shapes=[
            pltpu.VMEM((2, sizes, rows, LANES), f32),
            pltpu.VMEM((2, rows, sizes), f32),
            pltpu.SemaphoreType.DMA((2,)),
            pltpu.SemaphoreType.DMA((4,)),
            pltpu.SemaphoreType.DMA((4,)),
        ],
        compiler_params=pltpu.CompilerParams(collective_id=0, has_side_effects=True),
        name="halo",
    )(dust, pair_table, pair_rate.reshape(pairs // LANES, LANES))
    new_dust, _ = pl.pallas_call(
        functools.partial(collide_kernel, n_rad, n_pol),
        out_shape=(like(sizes, rows, tile), like(sizes, span, LANES)),
        in_specs=[ANY] * 3 + [VMEM] * 2 + [SMEM] * 5 + [VMEM],
        out_specs=(ANY, ANY),
        scratch_shapes=[pltpu.VMEM((pieces, sizes, 2 * SUB, LANES), f32)]
        + [pltpu.VMEM((sizes * span, LANES), f32)] * 5
        + [
            pltpu.VMEM((span, sizes, LANES), f32),
            pltpu.VMEM((sizes * span, LANES), f32),
            pltpu.SemaphoreType.DMA((3 * pieces,)),
            pltpu.SemaphoreType.DMA((4,)),
            pltpu.SemaphoreType.DMA((4 * pieces,)),
        ],
        name="collide",
    )(
        dust, below, above, left, right, drift_courant, mixing,
        sources.reshape(pairs), targets.reshape(pairs), pair_rate, loss,
    )
    heating = pl.pallas_call(
        functools.partial(heat_kernel, n_rad),
        out_shape=like(CH, rows, tile),
        in_specs=[ANY] + [VMEM] * 3,
        out_specs=VMEM,
        scratch_shapes=[
            pltpu.VMEM((rows, sizes, tile), f32),
            pltpu.VMEM((rows, bands, tile), f32),
            pltpu.VMEM((rows, 2 * bands, tile), bf16),
            pltpu.VMEM((rows, bands), f32),
            pltpu.VMEM((n_rad - 1, rows, bands), f32),
            pltpu.SemaphoreType.DMA((rows,)),
            pltpu.SemaphoreType.DMA,
            pltpu.SemaphoreType.DMA,
        ],
        compiler_params=pltpu.CompilerParams(collective_id=1, has_side_effects=True),
        name="heat",
    )(new_dust, absorption, stellar_flux.reshape(1, bands), band_channel.reshape(1, bands))
    return new_dust, heating


def solution(mesh):
    placed = (P(None, "pol", "rad"), P(), P(), P(), P(), P(), P(), P())
    return jax.shard_map(
        shards,
        mesh=mesh,
        in_specs=placed,
        out_specs=(P(None, "pol", "rad"), P(None, "pol", "rad")),
        check_vma=False,
    )
```
